32 devices in a mesh: dp: 8 (over y, x, core), fsdp: 4 (over z).
Axes of the slice: x: 2, y: 2, z: 4, core: 2. Of those that a mesh axis runs over, the one named last changes fastest.
Arguments:
- tokens: bfloat16 [16384, 1024], P(('dp', 'fsdp')), may hold values from -20 to 20
- w_qkv: bfloat16 [1024, 3072], P('fsdp'), may hold values from -0.1875 to 0.1875
- w_out: bfloat16 [1024, 1024], P('fsdp'), may hold values from -0.1875 to 0.1875
- doc_blocks: int32 [32, 4], P(('dp', 'fsdp')), may hold values from 0 to 1, never falling along the last dimension, each value on 1 to 3 neighbouring positions
- cotangent: bfloat16 [16384, 1024], P(('dp', 'fsdp')), may hold values from -6 to 6
Outputs:
- output: bfloat16 [16384, 1024], P(('dp', 'fsdp'))
- grad_tokens: bfloat16 [16384, 1024], P(('dp', 'fsdp'))
- grad_w_qkv: float32 [1024, 3072], P('fsdp')
- grad_w_out: float32 [1024, 1024], P('fsdp')
The draws below stay inside these ranges and needn't reach their ends.
Inputs may be any that keep to these rules, and one draw needn't show every extreme that they name: `doc_blocks`: ids never fall along a sequence; each of the 2 documents of a sequence covers 1 to 3 blocks.
All inputs are finite; a program needn't handle non-finite values.
Results may differ from the reference program's by a relative error of at most 0.012.
Values may be sent and summed in bfloat16 or wider, within the bound.
A program may use at most 128 MiB of HBM per device.

```python
import math
import jax
import jax.numpy as jnp
import numpy as np
from jax import lax

D = 1024
H = 8
HD = 128
TOK_DEV = 512
HW = 1024
NB = 4
DOCS = 2
MOST = 3
SEQS = 32
TOKENS = 16384


def draw_tokens(key, part):
    first = jax.random.fold_in(key, 0)
    values = jnp.clip(jax.random.normal(first, (TOKENS, D), jnp.float32), -6.0, 6.0)
    return values.astype(jnp.bfloat16)


def with_spikes(drawn, stream_key, source, target, shards_of, factor):
    owner, partner = [(jnp.arange(drawn.shape[dim]) // (drawn.shape[dim] // shards_of)).reshape([-1 if axis == dim else 1 for axis in range(drawn.ndim)]) for dim in (source, target)]
    chosen = jax.random.permutation(stream_key, shards_of)[partner]
    strong = (owner == chosen) | (owner == (partner + shards_of // 2) % shards_of)
    return jnp.where(strong, factor * drawn, drawn)


def steps_of(rng, dims, shards, least, top_value):
    level, own = 1.0, jax.random.fold_in(rng, 6)
    for dim, parts in shards:
        draws = jnp.exp(jax.random.uniform(jax.random.fold_in(own, dim), (parts,), jnp.float32, least / len(shards), top_value / len(shards)))
        level = level * jnp.repeat(draws, dims[dim] // parts).reshape([-1 if axis == dim else 1 for axis in range(len(dims))])
    return level


def length_profile(amount, total, reach, slope):
    portions = [(1 << 20) // math.isqrt(rank ** slope) + 1 for rank in range(2, amount + 1)]
    rest, given = total - reach - (amount - 1), [1] * (amount - 1)
    while rest > 0:
        candidates = [i for i in range(amount - 1) if given[i] < reach]
        pool, left = sum([portions[i] for i in candidates]), rest
        for i in candidates:
            extra = min(reach - given[i], max(1, left * portions[i] // pool), rest)
            given[i] = given[i] + extra
            rest = rest - extra
    return np.array([reach] + given)


def uneven_parts(key, number_of, total, reach, skew):
    if number_of == 2:
        one = jax.random.randint(key, (), max(1, total - reach), min(reach, total - 1) + 1)
        return jnp.stack([one, total - one])
    lengths = jnp.asarray(length_profile(number_of, total, reach, skew), jnp.int32)
    pairs = (number_of - 1) // 2
    giver, receiver = lengths[1:1 + 2 * pairs:2], lengths[2:2 + 2 * pairs:2]
    slack = jnp.minimum(giver - 1, reach - receiver)
    passed = jax.random.randint(jax.random.fold_in(key, 1), (pairs,), 0, 1 << 20) % (slack + 1)
    lengths = lengths.at[1:1 + 2 * pairs:2].set(giver - passed).at[2:2 + 2 * pairs:2].set(receiver + passed)
    return lengths[jax.random.permutation(jax.random.fold_in(key, 2), number_of)]


def centred(stream_key, shape, scale, reach, cuts=(), held_as=jnp.bfloat16):
    loudness = steps_of(stream_key, shape, cuts, -0.22, 0.18) if cuts else 1.0
    drawn = jax.random.normal(stream_key, shape, jnp.float32) * scale * loudness
    return jnp.minimum(jnp.maximum(drawn, -reach), reach).astype(held_as)


def noise_with(key, extent, spread, most, cuts, heavy, kind=jnp.bfloat16):
    entries = spread * jax.random.normal(key, extent, jnp.float32)
    if cuts:
        entries = entries * steps_of(key, extent, cuts, -0.22, 0.18)
    return jnp.clip(with_spikes(entries, jax.random.fold_in(key, 3), *heavy), -most, most).astype(kind)


def setup_inputs(seed: int = 0) -> dict:
    keys = jax.random.split(jax.random.key(seed), 6)
    tokens = draw_tokens(jax.random.fold_in(keys[5], 71), 0)
    w_qkv = centred(keys[1], (D, 3 * HW), D ** -0.5, 0.1875, ((0, 4),))
    w_out = centred(keys[2], (D, HW), HW ** -0.5, 0.1875, ((0, 4),))
    doc_blocks = jax.vmap(lambda own: jnp.searchsorted(jnp.cumsum(uneven_parts(own, DOCS, NB, MOST, 0)), jnp.arange(NB), side="right"))(jax.random.split(keys[3], SEQS)).reshape((SEQS, NB)).astype(jnp.int32)
    cotangent = noise_with(keys[4], (TOKENS, D), 1.0, 6.0, ((0, 32),), (0, 1, 32, 2.75))
    return {"tokens": tokens, "w_qkv": w_qkv, "w_out": w_out, "doc_blocks": doc_blocks, "cotangent": cotangent}


NEG_FILL = -1e+30

def row_mask(doc_ids, row_count):
    block_len = row_count // doc_ids.shape[0]
    doc_rows = jnp.repeat(doc_ids, block_len, total_repeat_length=row_count)
    position = jnp.arange(row_count, dtype=jnp.int32)
    causal = position[None, :] <= position[:, None]
    return causal & (doc_rows[None, :] == doc_rows[:, None])

def split_heads(matrix, head_count):
    return matrix.reshape(matrix.shape[0], head_count, matrix.shape[1] // head_count).astype(jnp.float32)

def attend_forward(query_rows, key_rows, value_rows, allowed, head_count):
    row_count = query_rows.shape[0]
    query_heads = split_heads(query_rows, head_count)
    key_heads = split_heads(key_rows, head_count)
    value_heads = split_heads(value_rows, head_count)
    score_scale = query_heads.shape[2] ** (-0.5)
    scores = jnp.einsum('qhd,khd->hqk', query_heads, key_heads, precision=lax.Precision.HIGHEST) * score_scale
    scores = jnp.where(allowed[None], scores, NEG_FILL)
    highest = lax.optimization_barrier(jnp.max(scores, axis=-1, keepdims=True))
    expvals = jnp.exp(scores - highest)
    attn_probs = expvals / lax.optimization_barrier(jnp.sum(expvals, axis=-1, keepdims=True))
    probs_half = attn_probs.astype(jnp.bfloat16)
    mixed = jnp.einsum('hqk,khd->qhd', probs_half.astype(jnp.float32), value_heads, precision=lax.Precision.HIGHEST)
    return (mixed.astype(jnp.bfloat16).reshape(row_count, -1), attn_probs, probs_half)

def attend_backward(query_rows, key_rows, value_rows, attn_probs, probs_half, grad_mixed, head_count):
    row_count = query_rows.shape[0]
    query_heads = split_heads(query_rows, head_count)
    key_heads = split_heads(key_rows, head_count)
    value_heads = split_heads(value_rows, head_count)
    grad_heads = split_heads(grad_mixed, head_count)
    score_scale = query_heads.shape[2] ** (-0.5)
    grad_probs = jnp.einsum('qhd,khd->hqk', grad_heads, value_heads, precision=lax.Precision.HIGHEST)
    grad_values = jnp.einsum('hqk,qhd->khd', probs_half.astype(jnp.float32), grad_heads, precision=lax.Precision.HIGHEST)
    inner = lax.optimization_barrier(jnp.sum(attn_probs * grad_probs, axis=-1, keepdims=True))
    grad_scores = (attn_probs * (grad_probs - inner)).astype(jnp.bfloat16).astype(jnp.float32)
    grad_queries = jnp.einsum('hqk,khd->qhd', grad_scores, key_heads, precision=lax.Precision.HIGHEST) * score_scale
    grad_keys = jnp.einsum('hqk,qhd->khd', grad_scores, query_heads, precision=lax.Precision.HIGHEST) * score_scale
    pieces_list = [grad_queries, grad_keys, grad_values]
    return jnp.concatenate([p.astype(jnp.bfloat16).reshape(row_count, -1) for p in pieces_list], axis=1)

def reference(tokens, w_qkv, w_out, doc_blocks, cotangent):
    seq_count = doc_blocks.shape[0]
    token_seqs = tokens.reshape(seq_count, TOK_DEV, D)
    grad_seqs = cotangent.reshape(seq_count, TOK_DEV, D)
    head_width = H * HD

    def one_sequence(carry, item):
        seq_rows, seq_grad, doc_ids = item
        allowed = row_mask(doc_ids, TOK_DEV)
        qkv = jnp.dot(seq_rows, w_qkv, preferred_element_type=jnp.float32).astype(jnp.bfloat16)
        query_rows = qkv[:, :head_width]
        key_rows = qkv[:, head_width:2 * head_width]
        value_rows = qkv[:, 2 * head_width:]
        mixed, attn_probs, probs_half = attend_forward(query_rows, key_rows, value_rows, allowed, H)
        output = jnp.dot(mixed, w_out.T, preferred_element_type=jnp.float32).astype(jnp.bfloat16)
        grad_mixed = jnp.dot(seq_grad, w_out, preferred_element_type=jnp.float32).astype(jnp.bfloat16)
        grad_qkv = attend_backward(query_rows, key_rows, value_rows, attn_probs, probs_half, grad_mixed, H)
        grad_tokens = jnp.dot(grad_qkv, w_qkv.T, preferred_element_type=jnp.float32).astype(jnp.bfloat16)
        sum_qkv = carry[0] + jnp.dot(seq_rows.T, grad_qkv, preferred_element_type=jnp.float32)
        sum_out = carry[1] + jnp.dot(seq_grad.T, mixed, preferred_element_type=jnp.float32)
        return ((sum_qkv, sum_out), (output, grad_tokens))
    start_sums = (jnp.zeros((D, 3 * head_width), jnp.float32), jnp.zeros((D, head_width), jnp.float32))
    sums_final, outputs = lax.scan(one_sequence, start_sums, (token_seqs, grad_seqs, doc_blocks))
    norm_factor = 1.0 / math.sqrt(TOKENS)
    output = outputs[0].reshape(TOKENS, D)
    grad_tokens = outputs[1].reshape(TOKENS, D)
    return (output, grad_tokens, sums_final[0] * norm_factor, sums_final[1] * norm_factor)
```

```python
import functools
import math

import jax
import jax.numpy as jnp
from jax import lax
from jax.experimental import pallas as pl
from jax.experimental.pallas import tpu as pltpu
from jax.sharding import PartitionSpec as P

H = 8


NEG_FILL = -1e30
CONTRACT_ROWS = (((0,), (0,)), ((), ()))
CONTRACT_COLS = (((1,), (1,)), ((), ()))


def row_mask(doc_ids, row_count):
    block_len = row_count // doc_ids.shape[0]
    doc_rows = jnp.repeat(doc_ids, block_len, total_repeat_length=row_count)
    position = jnp.arange(row_count, dtype=jnp.int32)
    causal = position[None, :] <= position[:, None]
    return causal & (doc_rows[None, :] == doc_rows[:, None])


def split_heads(matrix, head_count):
    return matrix.reshape(matrix.shape[0], head_count, matrix.shape[1] // head_count)


def attend_forward(query_rows, key_rows, value_rows, allowed, head_count):
    row_count = query_rows.shape[0]
    query_heads = split_heads(query_rows, head_count)
    key_heads = split_heads(key_rows, head_count)
    value_heads = split_heads(value_rows, head_count)
    score_scale = query_heads.shape[2] ** (-0.5)
    scores = (
        jnp.einsum("qhd,khd->hqk", query_heads, key_heads, preferred_element_type=jnp.float32)
        * score_scale
    )
    scores = jnp.where(allowed[None], scores, NEG_FILL)
    highest = jnp.max(scores, axis=-1, keepdims=True)
    expvals = jnp.exp(scores - highest)
    attn_probs = expvals / jnp.sum(expvals, axis=-1, keepdims=True)
    probs_half = attn_probs.astype(jnp.bfloat16)
    mixed = jnp.einsum("hqk,khd->qhd", probs_half, value_heads, preferred_element_type=jnp.float32)
    return (mixed.astype(jnp.bfloat16).reshape(row_count, -1), attn_probs, probs_half)


def attend_backward(
    query_rows, key_rows, value_rows, attn_probs, probs_half, grad_mixed, head_count
):
    row_count = query_rows.shape[0]
    query_heads = split_heads(query_rows, head_count)
    key_heads = split_heads(key_rows, head_count)
    value_heads = split_heads(value_rows, head_count)
    grad_heads = split_heads(grad_mixed, head_count)
    score_scale = query_heads.shape[2] ** (-0.5)
    grad_probs = jnp.einsum(
        "qhd,khd->hqk", grad_heads, value_heads, preferred_element_type=jnp.float32
    )
    grad_values = jnp.einsum(
        "hqk,qhd->khd", probs_half, grad_heads, preferred_element_type=jnp.float32
    )
    inner = jnp.sum(attn_probs * grad_probs, axis=-1, keepdims=True)
    grad_scores = (attn_probs * (grad_probs - inner)).astype(jnp.bfloat16)
    grad_queries = (
        jnp.einsum("hqk,khd->qhd", grad_scores, key_heads, preferred_element_type=jnp.float32)
        * score_scale
    )
    grad_keys = (
        jnp.einsum("hqk,qhd->khd", grad_scores, query_heads, preferred_element_type=jnp.float32)
        * score_scale
    )
    pieces_list = [grad_queries, grad_keys, grad_values]
    return jnp.concatenate(
        [p.astype(jnp.bfloat16).reshape(row_count, -1) for p in pieces_list], axis=1
    )


def body(tokens, w_qkv, w_out, doc_blocks, cotangent):
    row_count = tokens.shape[0]
    head_width = w_out.shape[1]
    head_count = H
    all_devices = lax.axis_size("dp") * lax.axis_size("fsdp")
    allowed = row_mask(doc_blocks[0], row_count)
    columns = tokens
    qkv = jnp.dot(
        columns,
        lax.all_gather(w_qkv, "fsdp", axis=0, tiled=True),
        preferred_element_type=jnp.float32,
    ).astype(jnp.bfloat16)
    query_rows = qkv[:, :head_width]
    key_rows = qkv[:, head_width : 2 * head_width]
    value_rows = qkv[:, 2 * head_width :]
    mixed, attn_probs, probs_half = attend_forward(
        query_rows, key_rows, value_rows, allowed, head_count
    )
    output = lax.dot_general(
        mixed,
        lax.all_gather(w_out, "fsdp", axis=0, tiled=True),
        CONTRACT_COLS,
        preferred_element_type=jnp.float32,
    )
    columns = cotangent
    grad_mixed = jnp.dot(
        columns,
        lax.all_gather(w_out, "fsdp", axis=0, tiled=True),
        preferred_element_type=jnp.float32,
    ).astype(jnp.bfloat16)
    output = output.astype(jnp.bfloat16)
    grad_qkv = attend_backward(
        query_rows, key_rows, value_rows, attn_probs, probs_half, grad_mixed, head_count
    )
    grad_tokens = lax.dot_general(
        grad_qkv,
        lax.all_gather(w_qkv, "fsdp", axis=0, tiled=True),
        CONTRACT_COLS,
        preferred_element_type=jnp.float32,
    )
    grad_tokens = grad_tokens.astype(jnp.bfloat16)
    first_term = lax.dot_general(
        tokens, grad_qkv, CONTRACT_ROWS, preferred_element_type=jnp.float32
    )
    second_term = lax.dot_general(
        cotangent, mixed, CONTRACT_ROWS, preferred_element_type=jnp.float32
    )
    partial_grad = lax.psum_scatter(
        jnp.concatenate([first_term, second_term], axis=1), "fsdp", scatter_dimension=0, tiled=True
    )
    summed = lax.psum(partial_grad, "dp")
    norm_factor = 1.0 / math.sqrt(row_count * all_devices)
    grad_w_qkv = summed[:, : 3 * head_width] * norm_factor
    grad_w_out = summed[:, 3 * head_width :] * norm_factor
    return (output, grad_tokens, grad_w_qkv, grad_w_out)


MESH = pl.DeviceIdType.MESH


class Place:
    def __init__(self, fsdp_size):
        self.d, self.f = lax.axis_index("dp"), lax.axis_index("fsdp")
        self.c = lax.rem(self.d, 2)
        chip = lax.div(self.d, 2)
        self.x, self.y = lax.rem(chip, 2), lax.div(chip, 2)
        self.dx = self.dp_of(self.y, 1 - self.x, self.c)
        self.dy = self.dp_of(1 - self.y, self.x, self.c)
        self.dd = self.dp_of(1 - self.y, 1 - self.x, self.c)
        self.dc = self.dp_of(self.y, self.x, 1 - self.c)
        self.n = fsdp_size

    def dp_of(self, y, x, c):
        return (y * 2 + x) * 2 + c

    def ahead(self, j):
        return lax.rem(self.f + j, self.n)

    def behind(self, j):
        return lax.rem(self.f + self.n - j, self.n)

    def barrier(self):
        sem = pltpu.get_barrier_semaphore()
        targets = [(self.dx, self.f), (self.dy, self.f), (self.dc, self.f)]
        targets += [(self.d, self.ahead(j)) for j in range(1, self.n)]
        for target in targets:
            pl.semaphore_signal(sem, inc=1, device_id=target, device_id_type=MESH)
        pl.semaphore_wait(sem, len(targets))


def remote(src, dst, send_sem, recv_sem, target):
    return pltpu.make_async_remote_copy(
        src_ref=src,
        dst_ref=dst,
        send_sem=send_sem,
        recv_sem=recv_sem,
        device_id=target,
        device_id_type=MESH,
    )


(
    GZ, GX, GY, GC, GXY, GYX, GCX, GCY, GCD, GCE,
    RC, PX, PY, QX, QY, RZ,
    SX, SY, SC, SXY, SYX, SCX, SCY, SCD, SCE,
) = (0, 3, 4, 5, 6, 7, 8, 9, 10, 11, 12, 13, 14, 15, 16, 17, 20, 21, 22, 23, 24, 25, 26, 27, 28)
KINDS = 29
LEAD = 3
PLAIN = (((1,), (0,)), ((), ()))


def add_half(left, right):
    return (left.astype(jnp.float32) + right.astype(jnp.float32)).astype(jnp.bfloat16)


def dot(left, right, dims=PLAIN):
    return lax.dot_general(left, right, dims, preferred_element_type=jnp.float32)


def layer_kernel(
    n,
    doc_ref,
    tok_any,
    cot_any,
    wq_any,
    wo_any,
    sumq_any,
    sumo_any,
    out_any,
    gt_any,
    tok,
    cot,
    tok_t,
    cot_t,
    w,
    bias,
    x,
    g,
    grads,
    core_sum,
    pair_x,
    pair_y,
    plane,
    z_terms,
    sums,
    result,
    send,
    recv,
    w_sem,
    in_sem,
    sum_sem,
    res_sem,
):
    me = Place(n)
    rows, feat = tok.shape
    share = w.shape[3]
    mid = share // 2
    size = w.shape[4] // 4
    wide = 3 * size
    block = feat // n
    low, high = pl.ds(0, mid), pl.ds(mid, mid)
    others = pl.ds(1, n - 1)

    def spot_of(r):
        return pl.ds(pl.multiple_of(me.ahead(r) * block, block), block)

    def w_load(h, p):
        if p == 3:
            src = wo_any.at[:, :, pl.ds(pl.multiple_of(h * size, size), size)]
        else:
            first = pl.multiple_of(p * H * size + h * size, size)
            src = wq_any.at[:, :, pl.ds(first, size)]
        dst = w.at[h, 0, :, :, pl.ds(p * size, size)]
        return pltpu.make_async_copy(src, dst, w_sem.at[h, p])

    def in_load(i, r):
        src, dst = ((tok_any, tok), (cot_any, cot))[i]
        return pltpu.make_async_copy(
            src.at[:, spot_of(r)], dst.at[:, pl.ds(r * block, block)], in_sem.at[i, r]
        )

    def sum_store(h, p):
        if p == 3:
            dst = sumo_any.at[:, :, pl.ds(pl.multiple_of(h * size, size), size)]
        else:
            first = pl.multiple_of(p * H * size + h * size, size)
            dst = sumq_any.at[:, :, pl.ds(first, size)]
        return pltpu.make_async_copy(
            sums.at[h, :, :, pl.ds(p * size, size)], dst, sum_sem.at[h, p]
        )

    def res_store(i, r):
        dst = (gt_any, out_any)[i].at[:, spot_of(r)]
        return pltpu.make_async_copy(result.at[i, r], dst, res_sem.at[i, r])

    def make(h, kind, src, dst, target):
        return remote(src, dst, send.at[h, kind], recv.at[h, kind], target)

    to_x, to_y, to_c = (me.dx, me.f), (me.dy, me.f), (me.dc, me.f)

    def copy(h, kind, j=0):
        if kind == GZ:
            return make(
                h, GZ + j - 1, w.at[h, 0, me.d], w.at[h, n - j, me.d], (me.d, me.ahead(j))
            )
        if kind == RZ:
            return make(h, RZ + j - 1, plane.at[h, j], z_terms.at[h, j - 1], (me.d, me.ahead(j)))
        if kind == RC:
            return make(h, kind, grads.at[h, :, :, :, 1 - me.c], core_sum.at[h], to_c)
        if kind == PX:
            src = core_sum.at[h, :, :, 1 - me.x, low]
            return make(h, kind, src, pair_x.at[h], to_x)
        if kind == PY:
            src = core_sum.at[h, :, 1 - me.y, :, high]
            return make(h, kind, src, pair_y.at[h], to_y)
        if kind == QX:
            return make(h, kind, pair_x.at[h, :, 1 - me.y], plane.at[h, :, low], to_y)
        if kind == QY:
            return make(h, kind, pair_y.at[h, :, 1 - me.x], plane.at[h, :, high], to_x)
        if kind < RC:
            def at(d, part=None):
                return w.at[h, others, d] if part is None else w.at[h, others, d, part]
        else:
            def at(d, part=None):
                return sums.at[h, d] if part is None else sums.at[h, d, part]
        spot, target = {
            GX: (at(me.d), to_x),
            GY: (at(me.d), to_y),
            GC: (at(me.d), to_c),
            GXY: (at(me.dx, low), to_y),
            GYX: (at(me.dy, high), to_x),
            GCX: (at(me.dx), to_c),
            GCY: (at(me.dy), to_c),
            GCD: (at(me.dd, low), to_c),
            GCE: (at(me.dd, high), to_c),
        }[kind if kind < RC else kind - SX + GX]
        return make(h, kind, spot, spot, target)

    def spread(h, base):
        for kind in (GX, GY, GC):
            copy(h, base + kind).start()

    def forward(h, base):
        copy(h, base + GX).wait_recv()
        copy(h, base + GXY).start()
        copy(h, base + GCX).start()
        copy(h, base + GY).wait_recv()
        copy(h, base + GYX).start()
        copy(h, base + GCY).start()

    def across(h, base):
        copy(h, base + GXY).wait_recv()
        copy(h, base + GCD).start()
        copy(h, base + GYX).wait_recv()
        copy(h, base + GCE).start()

    def collect(h, base):
        for kind in (GC, GCX, GCY, GCD, GCE):
            copy(h, base + kind).wait_recv()

    def gather_spread(h):
        for j in range(1, n):
            copy(h, GZ, j).wait_recv()
        spread(h, 0)

    def gather_forward(h):
        forward(h, 0)

    def gather_across(h):
        across(h, 0)

    def project(h):
        collect(h, 0)
        x[:, :wide] = dot(
            tok[...], w[h, :, :, :, :wide].reshape(feat, wide)
        ).astype(jnp.bfloat16)
        x[:, wide:] = dot(
            cot[...], w[h, :, :, :, wide:].reshape(feat, size)
        ).astype(jnp.bfloat16)

    def attend(h):
        scale = size ** (-0.5)
        half = rows // 2
        parts = []
        for first, keys in ((0, half), (half, rows)):
            mine = slice(first, first + half)
            q, k = x[mine, :size], x[:keys, size : 2 * size]
            v, gm = x[:keys, 2 * size : wide], x[mine, wide:]
            scores = dot(q, k, CONTRACT_COLS) * scale + bias[mine, :keys]
            expvals = jnp.exp(scores - jnp.max(scores, axis=-1, keepdims=True))
            probs = expvals * (1.0 / jnp.sum(expvals, axis=-1, keepdims=True))
            probs_half = probs.astype(jnp.bfloat16)
            g[h, mine, wide:] = dot(probs_half, v).astype(jnp.bfloat16)
            grad_probs = dot(gm, v, CONTRACT_COLS)
            inner = jnp.sum(probs * grad_probs, axis=-1, keepdims=True)
            grad_scores = (probs * (grad_probs - inner)).astype(jnp.bfloat16)
            g[h, mine, :size] = (dot(grad_scores, k) * scale).astype(jnp.bfloat16)
            parts.append((dot(grad_scores, q, CONTRACT_ROWS), dot(probs_half, gm, CONTRACT_ROWS)))
        for i, factor in ((0, scale), (1, 1.0)):
            cols = slice((i + 1) * size, (i + 2) * size)
            early, late = parts[0][i], parts[1][i]
            g[h, :half, cols] = ((early + late[:half]) * factor).astype(jnp.bfloat16)
            g[h, half:, cols] = (late[half:] * factor).astype(jnp.bfloat16)

    def weight_grad(h):
        def some(r, carry):
            part = pl.ds(pl.multiple_of(r * block, block), block)
            shape = (2, 2, 2, share)
            left = dot(tok_t[part, :], g[h, :, :wide]).astype(jnp.bfloat16)
            grads[h, r, :, :, :, :, :wide] = left.reshape(*shape, wide)
            right = dot(cot_t[part, :], g[h, :, wide:]).astype(jnp.bfloat16)
            grads[h, r, :, :, :, :, wide:] = right.reshape(*shape, size)
            return carry

        lax.fori_loop(0, n, some, 0)
        copy(h, RC).start()

    def core_add(h):
        copy(h, RC).wait_recv()

        def some(r, carry):
            core_sum[h, r] = add_half(grads[h, r, :, :, me.c], core_sum[h, r])
            return carry

        lax.fori_loop(0, n, some, 0)
        copy(h, PX).start()
        copy(h, PY).start()

    def pair_add(h):
        copy(h, PX).wait_recv()
        pair_x[h] = add_half(core_sum[h, :, :, me.x, :mid], pair_x[h])
        copy(h, QX).start()
        copy(h, PY).wait_recv()
        pair_y[h] = add_half(core_sum[h, :, me.y, :, mid:], pair_y[h])
        copy(h, QY).start()

    def plane_add(h):
        copy(h, QX).wait_recv()
        plane[h, :, :mid] = add_half(pair_x[h, :, me.y], plane[h, :, :mid])
        copy(h, QY).wait_recv()
        plane[h, :, mid:] = add_half(pair_y[h, :, me.x], plane[h, :, mid:])
        for j in range(1, n):
            copy(h, RZ, j).start()

    def line_add(h):
        total = plane[h, 0].astype(jnp.float32)
        for j in range(1, n):
            copy(h, RZ, j).wait_recv()
            total = total + z_terms[h, j - 1].astype(jnp.float32)
        sums[h, me.d] = total.astype(jnp.bfloat16)
        spread(h, SX - GX)

    def sum_forward(h):
        forward(h, SX - GX)

    def sum_across(h):
        across(h, SX - GX)

    def sum_finish(h):
        collect(h, SX - GX)
        for p in range(4):
            sum_store(h, p).start()

    def token_piece(r):
        total = None
        for h in range(H):
            right = w[h, r, :, :, :wide].reshape(block, wide)
            part = dot(g[h, :, :wide], right, CONTRACT_COLS)
            total = part if total is None else total + part
        result[0, r] = total.astype(jnp.bfloat16)
        res_store(0, r).start()

    def output_piece(r):
        total = None
        for h in range(H):
            right = w[h, r, :, :, wide:].reshape(block, size)
            part = dot(g[h, :, wide:], right, CONTRACT_COLS)
            total = part if total is None else total + part
        result[1, r] = total.astype(jnp.bfloat16)
        res_store(1, r).start()

    for h in range(H):
        for p in range(4):
            w_load(h, p).start()
    for i in range(2):
        for r in range(n):
            in_load(i, r).start()
    me.barrier()
    for h in range(H):
        for p in range(4):
            w_load(h, p).wait()
        for j in range(1, n):
            copy(h, GZ, j).start()
    docs = [doc_ref[0, b] for b in range(doc_ref.shape[1])]
    length = rows // len(docs)

    def doc_of(index):
        found = jnp.full(index.shape, docs[0], jnp.int32)
        for b in range(1, len(docs)):
            found = jnp.where(index >= b * length, docs[b], found)
        return found

    def fill(i, carry):
        first = pl.multiple_of(i * 128, 128)
        row = lax.broadcasted_iota(jnp.int32, (128, 1), 0) + first
        col = lax.broadcasted_iota(jnp.int32, (1, rows), 1)
        allowed = (col <= row) & (doc_of(row) == doc_of(col))
        bias[pl.ds(first, 128), :] = jnp.where(allowed, 0.0, NEG_FILL)
        return carry

    lax.fori_loop(0, rows // 128, fill, 0)
    for i in range(2):
        for r in range(n):
            in_load(i, r).wait()

    def turn(i, carry):
        part = pl.ds(pl.multiple_of(i * 128, 128), 128)
        tok_t[part, :] = tok[:, part].T
        cot_t[part, :] = cot[:, part].T
        return carry

    lax.fori_loop(0, feat // 128, turn, 0)

    stages = (
        (0, H, gather_spread),
        (1, H, gather_forward),
        (2, H, gather_across),
        (LEAD + 1, H, core_add),
        (LEAD, H, project),
        (LEAD + 2, H, pair_add),
        (LEAD + 4, H, plane_add),
        (LEAD, H, attend),
        (LEAD + 5, H, line_add),
        (LEAD + 6, H, sum_forward),
        (LEAD, H, weight_grad),
        (LEAD + 7, H, sum_across),
        (LEAD + H, n, token_piece),
        (LEAD + H, n, output_piece),
        (LEAD + 8, H, sum_finish),
    )

    def step(t, carry):
        for after, count, stage in stages:
            k = t - after
            pl.when((k >= 0) & (k < count))(functools.partial(stage, k))
        return carry

    lax.fori_loop(0, LEAD + 8 + H, step, 0)

    def finish(h, carry):
        for kind in range(KINDS):
            if GZ <= kind < GX:
                copy(h, GZ, kind - GZ + 1).wait_send()
            elif RZ <= kind < SX:
                copy(h, RZ, kind - RZ + 1).wait_send()
            else:
                copy(h, kind).wait_send()
        for p in range(4):
            sum_store(h, p).wait()
        return carry

    lax.fori_loop(0, H, finish, 0)
    for i in range(2):
        for r in range(n):
            res_store(i, r).wait()


def layer(n, tokens, cotangent, w_qkv, w_out, doc_blocks):
    rows, feat = tokens.shape
    shard, head_width = w_out.shape
    share, size = shard // 8, head_width // H
    wide = 4 * size
    half = jnp.bfloat16
    anywhere = pl.BlockSpec(memory_space=pl.ANY)
    w_qkv = w_qkv.reshape(8, share, 3 * head_width)
    w_out = w_out.reshape(8, share, head_width)
    sumq, sumo, output, grad_tokens = pl.pallas_call(
        functools.partial(layer_kernel, n),
        out_shape=[
            jax.ShapeDtypeStruct(w_qkv.shape, half),
            jax.ShapeDtypeStruct(w_out.shape, half),
            jax.ShapeDtypeStruct((rows, feat), half),
            jax.ShapeDtypeStruct((rows, feat), half),
        ],
        in_specs=[pl.BlockSpec(memory_space=pltpu.SMEM)] + [anywhere] * 4,
        out_specs=[anywhere] * 4,
        scratch_shapes=[
            pltpu.VMEM((rows, feat), half),
            pltpu.VMEM((rows, feat), half),
            pltpu.VMEM((feat, rows), half),
            pltpu.VMEM((feat, rows), half),
            pltpu.VMEM((H, n, 8, share, wide), half),
            pltpu.VMEM((rows, rows), jnp.float32),
            pltpu.VMEM((rows, wide), half),
            pltpu.VMEM((H, rows, wide), half),
            pltpu.VMEM((H, n, 2, 2, 2, share, wide), half),
            pltpu.VMEM((H, n, 2, 2, share, wide), half),
            pltpu.VMEM((H, n, 2, share // 2, wide), half),
            pltpu.VMEM((H, n, 2, share // 2, wide), half),
            pltpu.VMEM((H, n, share, wide), half),
            pltpu.VMEM((H, n - 1, share, wide), half),
            pltpu.VMEM((H, 8, share, wide), half),
            pltpu.VMEM((2, n, rows, feat // n), half),
            pltpu.SemaphoreType.DMA((H, KINDS)),
            pltpu.SemaphoreType.DMA((H, KINDS)),
            pltpu.SemaphoreType.DMA((H, 4)),
            pltpu.SemaphoreType.DMA((2, n)),
            pltpu.SemaphoreType.DMA((H, 4)),
            pltpu.SemaphoreType.DMA((2, n)),
        ],
        compiler_params=pltpu.CompilerParams(
            collective_id=0, has_side_effects=True, vmem_limit_bytes=60 << 20
        ),
        name="layer",
    )(doc_blocks, tokens, cotangent, w_qkv, w_out)
    return sumq.reshape(shard, 3 * head_width), sumo.reshape(shard, head_width), output, grad_tokens


def chip_body(tokens, w_qkv, w_out, doc_blocks, cotangent):
    n = lax.axis_size("fsdp")
    all_devices = lax.axis_size("dp") * n
    sumq, sumo, output, grad_tokens = layer(n, tokens, cotangent, w_qkv, w_out, doc_blocks)
    norm_factor = 1.0 / math.sqrt(tokens.shape[0] * all_devices)
    grad_w_qkv = sumq.astype(jnp.float32) * norm_factor
    grad_w_out = sumo.astype(jnp.float32) * norm_factor
    return (output, grad_tokens, grad_w_qkv, grad_w_out)


def solution(mesh):
    placed = (
        P(("dp", "fsdp"), None),
        P("fsdp", None),
        P("fsdp", None),
        P(("dp", "fsdp"), None),
        P(("dp", "fsdp"), None),
    )
    in_plane = mesh.shape["dp"] == 8 and mesh.shape["fsdp"] == 4
    return jax.shard_map(
        chip_body if in_plane else body,
        mesh=mesh,
        in_specs=placed,
        out_specs=(
            P(("dp", "fsdp"), None),
            P(("dp", "fsdp"), None),
            P("fsdp", None),
            P("fsdp", None),
        ),
        check_vma=False,
    )
```
